32 devices in a mesh: dp: 2 (over y), head: 16 (over z, x, core).
Axes of the slice: x: 2, y: 2, z: 4, core: 2. Of those that a mesh axis runs over, the one named last changes fastest.
Arguments:
- head_ids: int32 [2, 2048, 8], P('dp', 'head'), may hold values from 0 to 63, as said below
- query_slots: bfloat16 [2, 2048, 8, 128], P('dp', 'head'), may hold values from -300 to 300
- key_slots: bfloat16 [2, 2048, 8, 128], P('dp', 'head'), may hold values from -13 to 13
- value_slots: bfloat16 [2, 2048, 8, 128], P('dp', 'head'), may hold values from -5 to 5
- gate_logits: float32 [2, 2048, 8], P('dp', 'head'), may hold values from -8 to 310
- sink_logits: float32 [64], P('head'), may hold values from 1 to 6
- out_grad: bfloat16 [2, 2048, 8, 128], P('dp', 'head'), may hold values from -6 to 6
Outputs:
- mixed: bfloat16 [2, 2048, 8, 128], P('dp', 'head')
- query_grad: bfloat16 [2, 2048, 8, 128], P('dp', 'head')
- key_grad: bfloat16 [2, 2048, 8, 128], P('dp', 'head')
- value_grad: bfloat16 [2, 2048, 8, 128], P('dp', 'head')
- gate_grad: float32 [2, 2048, 8], P('dp', 'head')
- sink_grad: float32 [64], P('head')
The draws below stay inside these ranges and needn't reach their ends.
Inputs may be any that keep to these rules, and one draw needn't show every extreme that they name: `head_ids`: each token names 8 different heads. Among the 128 tokens of one device no head is named more than 32 times, and in every group one head is named exactly 32 times by the tokens of every device of that group.
All inputs are finite; a program needn't handle non-finite values.
Results may differ from the reference program's by a relative error of at most 0.023.
Values may be sent and summed in bfloat16 or wider, within the bound.
No kernel may reach another device: no remote copies, remote signals or barrier semaphores. Data moves between devices by JAX's collectives and lax.ppermute only.
A program may use at most 64 MiB of HBM per device.

```python
import math
import jax
import jax.numpy as jnp
from jax import lax

HEADS = 64
HDIM = 128
TOPK = 8
TOK_DEV = 128
GROUPS = 2
SEQ = 2048
SLOT = 32
CAP = 512


def route_block(block_key, hot_head):
    key_order, key_spread, key_others, key_roll = jax.random.split(block_key, 4)
    token_order = jax.random.permutation(key_order, TOK_DEV).astype(jnp.int32)
    rank_of = jnp.zeros((TOK_DEV,), jnp.int32).at[token_order].set(jnp.arange(TOK_DEV, dtype=jnp.int32))
    has_hot = (rank_of < SLOT).astype(jnp.int32)
    needed = TOPK - has_hot
    begin_at = jnp.cumsum(needed) - needed
    spread = jax.random.randint(key_spread, (), HEADS // 2, HEADS)
    others = jax.random.permutation(key_others, HEADS - 1).astype(jnp.int32)
    others = others + (others >= hot_head).astype(jnp.int32)
    column = jnp.arange(TOPK, dtype=jnp.int32)
    pick_index = jnp.mod(begin_at[:, None] + column[None, :] - has_hot[:, None], spread)
    picked = others[pick_index]
    chosen = jnp.where((has_hot[:, None] == 1) & (column[None, :] == 0), hot_head, picked)
    shift_by = jax.random.randint(key_roll, (TOK_DEV, 1), 0, TOPK)
    rolled = jnp.mod(column[None, :] + shift_by, TOPK)
    return jnp.take_along_axis(chosen, rolled, axis=1).astype(jnp.int32)


def route_group(group_key):
    key_hot, key_blocks = jax.random.split(group_key)
    hot_head = jax.random.randint(key_hot, (), 0, HEADS)
    block_keys = jax.random.split(key_blocks, SEQ // TOK_DEV)
    blocks_all = jax.vmap(route_block, in_axes=(0, None))(block_keys, hot_head)
    return blocks_all.reshape(SEQ, TOPK)


def route_ids(key):
    base_key = jax.random.fold_in(key, 11)
    return jax.vmap(route_group)(jax.random.split(base_key, GROUPS))


def draw_head_ids(key, part):
    return route_ids(key)


def slot_vectors(key):
    base_key = jax.random.fold_in(key, 23)
    key_key, key_query = jax.random.split(base_key, 2)
    dims_all = (GROUPS, SEQ, TOPK, HDIM)
    key_base = jnp.clip(jax.random.normal(key_key, dims_all, jnp.float32), -4.0, 4.0)
    queries = jnp.clip(1.5 * jax.random.normal(key_query, dims_all, jnp.float32), -9.0, 9.0)
    return (queries, key_base)


def draw_query_slots(key, part):
    return slot_vectors(key)[0].astype(jnp.bfloat16)


def draw_key_slots(key, part):
    return slot_vectors(key)[1].astype(jnp.bfloat16)


def draw_gate_logits(key, part):
    key_base = jax.random.fold_in(jax.random.fold_in(key, 31), 0)
    dims_all = (GROUPS, SEQ, TOPK)
    return jnp.clip(1.5 * jax.random.normal(key_base, dims_all, jnp.float32), -8.0, 8.0)


def level_of(stream_key, extent, cuts, low, top_value):
    factor_of = 1.0
    for dim, blocks in cuts:
        draws = jax.random.uniform(jax.random.fold_in(jax.random.fold_in(stream_key, 6), dim), (blocks,), jnp.float32, low / len(cuts), top_value / len(cuts))
        factor_of = factor_of * jnp.repeat(jnp.exp(draws), extent[dim] // blocks).reshape((-1,) + (1,) * (len(extent) - 1 - dim))
    return factor_of


def bell_draw(rng, extent, scale, reach, cuts=(), kind=jnp.bfloat16):
    gain = level_of(rng, extent, cuts, -0.22, 0.18) if cuts else 1.0
    drawn = jax.random.normal(rng, extent, jnp.float32) * scale * gain
    return jnp.minimum(jnp.maximum(drawn, -reach), reach).astype(kind)


def setup_inputs(seed: int = 0) -> dict:
    key_list = jax.random.split(jax.random.key(seed), 8)
    return {
        "head_ids": draw_head_ids(jax.random.fold_in(key_list[7], 71), 0),
        "query_slots": draw_query_slots(jax.random.fold_in(key_list[7], 71), 0),
        "key_slots": draw_key_slots(jax.random.fold_in(key_list[7], 71), 0),
        "value_slots": bell_draw(key_list[3], (GROUPS, SEQ, TOPK, HDIM), 1.0, 5.0, ((0, 2), (1, 16))),
        "gate_logits": draw_gate_logits(jax.random.fold_in(key_list[7], 71), 0),
        "sink_logits": jnp.clip(1.0 + 5.0 * jax.random.uniform(key_list[5], (HEADS,), jnp.float32) ** level_of(key_list[5], (HEADS,), ((0, 16),), -0.2, 0.2), 1.0, 6.0),
        "out_grad": bell_draw(key_list[6], (GROUPS, SEQ, TOPK, HDIM), 1.0, 6.0, ((0, 2), (1, 16))),
    }


masked_value = -1e+30

def head_terms(head_flat, query_flat, key_flat, value_flat, cot_flat, sink_value, head):
    index_list = jnp.argsort((head_flat != head).astype(jnp.int32), stable=True)[:CAP].astype(jnp.int32)
    live_rows = head_flat[index_list] == head
    position = index_list // TOPK
    query_rows = query_flat[index_list]
    key_rows = key_flat[index_list]
    value_rows = value_flat[index_list]
    cot_rows = jnp.where(live_rows[:, None], cot_flat[index_list], jnp.zeros((), jnp.bfloat16))
    scale = 1.0 / math.sqrt(HDIM)
    scores = scale * jnp.dot(query_rows, key_rows.T, preferred_element_type=jnp.float32)
    allowed = live_rows[:, None] & live_rows[None, :] & (position[None, :] <= position[:, None])
    masked = jnp.where(allowed, scores, masked_value)
    row_max = jnp.maximum(lax.optimization_barrier(jnp.max(masked, axis=1)), sink_value)
    row_sum = jnp.exp(sink_value - row_max) + lax.optimization_barrier(jnp.sum(jnp.where(allowed, jnp.exp(masked - row_max[:, None]), 0.0), axis=1))
    row_lse = row_max + jnp.log(row_sum)
    probability = jnp.where(allowed, jnp.exp(scores - row_lse[:, None]), 0.0)
    weights = probability.astype(jnp.bfloat16)
    head_out = jnp.dot(weights, value_rows, preferred_element_type=jnp.float32).astype(jnp.bfloat16)
    deltas = lax.optimization_barrier(jnp.sum(cot_rows.astype(jnp.float32) * head_out.astype(jnp.float32), axis=1))
    dprob = jnp.dot(cot_rows, value_rows.T, preferred_element_type=jnp.float32)
    dscore = (probability * (dprob - deltas[:, None])).astype(jnp.bfloat16)
    query_grad = (scale * jnp.dot(dscore, key_rows, preferred_element_type=jnp.float32)).astype(jnp.bfloat16)
    key_grad = (scale * jnp.dot(dscore.T, query_rows, preferred_element_type=jnp.float32)).astype(jnp.bfloat16)
    value_grad = jnp.dot(weights.T, cot_rows, preferred_element_type=jnp.float32).astype(jnp.bfloat16)
    sink_grad = -jnp.sum(jnp.exp(sink_value - row_lse) * deltas)
    return (index_list, live_rows, head_out, query_grad, key_grad, value_grad, sink_grad)

def group_terms(head_flat, query_flat, key_flat, value_flat, cot_flat, sink_logits):

    def per_head(carry, head):
        out_acc, qgrad_acc, kgrad_acc, vgrad_acc = carry
        index_list, live_rows, head_out, query_grad, key_grad, value_grad, sink_grad = head_terms(head_flat, query_flat, key_flat, value_flat, cot_flat, sink_logits[head], head)

        def add_to(total, values):
            return total.at[index_list].add(jnp.where(live_rows[:, None], values.astype(jnp.float32), jnp.zeros((), jnp.float32)))
        return ((add_to(out_acc, head_out), add_to(qgrad_acc, query_grad), add_to(kgrad_acc, key_grad), add_to(vgrad_acc, value_grad)), sink_grad)
    zeros_all = jnp.zeros((SEQ * TOPK, HDIM), jnp.float32)
    totals, sink_grads = lax.scan(per_head, (zeros_all, zeros_all, zeros_all, zeros_all), jnp.arange(HEADS, dtype=jnp.int32))
    return tuple((item.astype(jnp.bfloat16) for item in totals)) + (sink_grads,)

def reference(head_ids, query_slots, key_slots, value_slots, gate_logits, sink_logits, out_grad):
    gate_probs = jax.nn.softmax(gate_logits, axis=-1)
    cotangent = (gate_probs[..., None] * out_grad.astype(jnp.float32)).astype(jnp.bfloat16)

    def one_group(group):
        return group_terms(head_ids[group].reshape(-1), query_slots[group].reshape(-1, HDIM), key_slots[group].reshape(-1, HDIM), value_slots[group].reshape(-1, HDIM), cotangent[group].reshape(-1, HDIM), sink_logits)
    head_out, query_grad, key_grad, value_grad, sink_grads = lax.map(one_group, jnp.arange(GROUPS, dtype=jnp.int32))
    full_shape = (GROUPS, SEQ, TOPK, HDIM)
    head_out = head_out.reshape(full_shape)
    mixed = (gate_probs[..., None] * head_out.astype(jnp.float32)).astype(jnp.bfloat16)
    gate_sum = lax.optimization_barrier(jnp.sum(out_grad.astype(jnp.float32) * head_out.astype(jnp.float32), axis=-1))
    gate_grad = gate_probs * (gate_sum - lax.optimization_barrier(jnp.sum(gate_probs * gate_sum, axis=-1, keepdims=True)))
    sink_grad = lax.optimization_barrier(jnp.sum(sink_grads, axis=0))
    return (mixed, query_grad.reshape(full_shape), key_grad.reshape(full_shape), value_grad.reshape(full_shape), gate_grad, sink_grad)
```

```python
import functools
import math

import jax
import jax.numpy as jnp
from jax import lax
from jax.experimental import pallas as pl
from jax.experimental.pallas import tpu as pltpu
from jax.sharding import PartitionSpec as P

SLOT = 32
INFO = 16
MASKED = -1e30


def dot(a, b, dims):
    return lax.dot_general(a, b, (dims, ((), ())), preferred_element_type=jnp.float32)


def pack_kernel(heads, local_heads, dests, ids_ref, q_ref, k_ref, v_ref, c_ref, out_ref, target_ref, count_ref):
    step = pl.program_id(0)
    rows = ids_ref.shape[1]
    width = local_heads * SLOT

    @pl.when(step == 0)
    def _():
        lower = lax.broadcasted_iota(jnp.int32, (128, 128), 0)
        upper = lax.broadcasted_iota(jnp.int32, (128, 128), 1)
        before = jnp.where(lower < upper, 1.0, 0.0).astype(jnp.bfloat16)
        running = jnp.zeros((heads, 1), jnp.float32)
        for start in range(0, rows, 128):
            ids = ids_ref[:, start : start + 128]
            named = jnp.where(lax.broadcasted_iota(jnp.int32, (heads, 128), 0) == ids, 1.0, 0.0)
            earlier = dot(named.astype(jnp.bfloat16), before, ((1,), (0,))) + running
            place = jnp.sum(named * earlier, axis=0, keepdims=True)
            target_ref[:, start : start + 128] = ids * SLOT + place.astype(jnp.int32)
            running = running + jnp.sum(named, axis=1, keepdims=True)
        count_ref[...] = jnp.broadcast_to(running, (heads, 128))

    chunk = dests * width
    row = lax.broadcasted_iota(jnp.int32, (chunk, rows), 0) + step * chunk
    pick = jnp.where(row == target_ref[...], 1.0, 0.0).astype(jnp.bfloat16)
    for pair, refs in enumerate(((q_ref, k_ref), (v_ref, c_ref))):
        both = jnp.concatenate([refs[0][...], refs[1][...]], axis=1)
        res = dot(pick, both, ((1,), (0,))).astype(jnp.bfloat16)
        for part in range(2):
            start = (2 * pair + part) * width
            out_ref[:, start : start + width, :] = res[:, part * 128 : part * 128 + 128].reshape(dests, width, 128)
    line = lax.broadcasted_iota(jnp.int32, (dests * INFO, heads), 0)
    head = lax.broadcasted_iota(jnp.int32, (dests * INFO, heads), 1)
    wanted = (step * dests + line // INFO) * local_heads + line % INFO
    take = jnp.where((wanted == head) & (line % INFO < local_heads), 1.0, 0.0).astype(jnp.bfloat16)
    info = dot(take, count_ref[...].astype(jnp.bfloat16), ((1,), (0,)))
    out_ref[:, 4 * width :, :] = info.astype(jnp.bfloat16).reshape(dests, INFO, 128)


def attend_kernel(local_heads, block, sink_ref, recv_ref, out_ref, term_ref, dk_ref, dv_ref):
    head = pl.program_id(0)
    devices = recv_ref.shape[0]
    width = local_heads * SLOT
    rows = devices * SLOT
    depth = recv_ref.shape[-1]
    scale = 1.0 / math.sqrt(depth)
    sink = sink_ref[head]

    def part(index, first, size):
        start = pl.multiple_of(index * width + head * SLOT, SLOT)
        begin, count = first // SLOT, size // SLOT
        return recv_ref[begin : begin + count, pl.ds(start, SLOT), :].reshape(size, depth)

    def put(index, first, value):
        start = pl.multiple_of(index * width + head * SLOT, SLOT)
        begin, count = first // SLOT, value.shape[0] // SLOT
        out_ref[begin : begin + count, pl.ds(start, SLOT), :] = value.reshape(count, SLOT, depth)

    info = recv_ref[:, 4 * width :, :].astype(jnp.float32)
    line = lax.broadcasted_iota(jnp.int32, info.shape, 1)
    count = jnp.sum(jnp.where(line == head, info, 0.0), axis=1, keepdims=True)
    slot = lax.broadcasted_iota(jnp.int32, (devices, SLOT, 128), 1).astype(jnp.float32)
    dead = jnp.where(slot < count, 0.0, MASKED).reshape(rows, 128)

    below = lax.broadcasted_iota(jnp.int32, (block, block), 0) <= lax.broadcasted_iota(jnp.int32, (block, block), 1)
    blocks = rows // block
    total = jnp.zeros((1, block), jnp.float32)
    for qb in range(blocks):
        query = part(0, qb * block, block)
        cot = part(3, qb * block, block)
        scores = []
        top = jnp.full((1, block), sink, jnp.float32)
        for kb in range(qb + 1):
            key = part(1, kb * block, block)
            bias = jnp.concatenate([dead[kb * block : (kb + 1) * block]] * (block // 128), axis=1)
            score = scale * dot(key, query, ((1,), (1,))) + bias
            if kb == qb:
                score = jnp.where(below, score, MASKED)
            scores.append(score)
            top = jnp.maximum(top, jnp.max(score, axis=0, keepdims=True))
        sink_part = jnp.exp(sink - top)
        run = sink_part
        for kb in range(qb + 1):
            scores[kb] = jnp.exp(scores[kb] - top)
            run = run + jnp.sum(scores[kb], axis=0, keepdims=True)
        inv = 1.0 / run
        head_out = jnp.zeros((depth, block), jnp.float32)
        delta = jnp.zeros((1, block), jnp.float32)
        terms = []
        for kb in range(qb + 1):
            value = part(2, kb * block, block)
            prob = scores[kb] * inv
            weights = prob.astype(jnp.bfloat16)
            head_out = head_out + dot(value, weights, ((0,), (0,)))
            vpart = dot(weights, cot, ((1,), (0,)))
            dv_ref[kb * block : (kb + 1) * block] = vpart if kb == qb else dv_ref[kb * block : (kb + 1) * block] + vpart
            term = prob * dot(value, cot, ((1,), (1,)))
            delta = delta + jnp.sum(term, axis=0, keepdims=True)
            scores[kb] = prob
            terms.append(term)
        put(0, qb * block, head_out.T.astype(jnp.bfloat16))
        query_grad = jnp.zeros((depth, block), jnp.float32)
        for kb in range(qb + 1):
            dscore = (terms[kb] - scores[kb] * delta).astype(jnp.bfloat16)
            query_grad = query_grad + dot(part(1, kb * block, block), dscore, ((0,), (0,)))
            kpart = dot(dscore, query, ((1,), (0,)))
            dk_ref[kb * block : (kb + 1) * block] = kpart if kb == qb else dk_ref[kb * block : (kb + 1) * block] + kpart
        put(1, qb * block, (scale * query_grad).T.astype(jnp.bfloat16))
        total = total - sink_part * inv * delta
    for kb in range(blocks):
        put(2, kb * block, (scale * dk_ref[kb * block : (kb + 1) * block]).astype(jnp.bfloat16))
        put(3, kb * block, dv_ref[kb * block : (kb + 1) * block].astype(jnp.bfloat16))
    term_ref[0] = jnp.broadcast_to(jnp.sum(total, axis=1, keepdims=True), (8, 128))


def unpack_kernel(width, target_ref, gate_ref, grad_ref, back_ref, mixed_ref, dq_ref, dk_ref, dv_ref, sum_ref):
    chunk = target_ref.shape[0]
    devices = back_ref.shape[0]
    slots = devices * width
    row = lax.broadcasted_iota(jnp.int32, (chunk, slots), 1)
    pick = jnp.where(row == target_ref[...], 1.0, 0.0).astype(jnp.bfloat16)

    def both(first):
        halves = [
            back_ref[:, index * width : (index + 1) * width, :].reshape(slots, 128) for index in (first, first + 1)
        ]
        return dot(pick, jnp.concatenate(halves, axis=1), ((1,), (0,)))

    forward = both(0)
    token_out = forward[:, :128]
    mixed_ref[...] = (gate_ref[...] * token_out).astype(jnp.bfloat16)
    sum_ref[...] = jnp.sum(grad_ref[...].astype(jnp.float32) * token_out, axis=1, keepdims=True)
    dq_ref[...] = forward[:, 128:].astype(jnp.bfloat16)
    backward = both(2)
    dk_ref[...] = backward[:, :128].astype(jnp.bfloat16)
    dv_ref[...] = backward[:, 128:].astype(jnp.bfloat16)


def per_device(head_ids, query_slots, key_slots, value_slots, gate_logits, sink_logits, out_grad):
    devices = lax.axis_size("head")
    local_heads = sink_logits.shape[0]
    heads = local_heads * devices
    tokens, slots = head_ids.shape[1:]
    depth = query_slots.shape[-1]
    rows = tokens * slots
    width = local_heads * SLOT
    ids = head_ids.reshape(1, rows)
    gate_probs = jax.nn.softmax(gate_logits[0], axis=-1)
    cotangent = (gate_probs[:, :, None] * out_grad[0].astype(jnp.float32)).astype(jnp.bfloat16)
    flat = [item.reshape(rows, depth) for item in (query_slots, key_slots, value_slots, cotangent)]
    dests = max(1, 512 // width)
    message = 4 * width + INFO
    whole = lambda shape: pl.BlockSpec(shape, lambda *_: (0,) * len(shape))
    send, target = pl.pallas_call(
        functools.partial(pack_kernel, heads, local_heads, dests),
        grid=(devices // dests,),
        in_specs=[whole((1, rows))] + [whole((rows, depth))] * 4,
        out_specs=[pl.BlockSpec((dests, message, depth), lambda i: (i, 0, 0)), whole((1, rows))],
        out_shape=[
            jax.ShapeDtypeStruct((devices, message, depth), jnp.bfloat16),
            jax.ShapeDtypeStruct((1, rows), jnp.int32),
        ],
        scratch_shapes=[pltpu.VMEM((heads, 128), jnp.float32)],
        name="pack",
    )(ids, *flat)
    recv = lax.all_to_all(send, "head", split_axis=0, concat_axis=0, tiled=True)
    capacity = devices * SLOT
    block = min(256, capacity)
    result, terms = pl.pallas_call(
        functools.partial(attend_kernel, local_heads, block),
        grid=(local_heads,),
        in_specs=[pl.BlockSpec(memory_space=pltpu.SMEM), whole((devices, message, depth))],
        out_specs=[whole((devices, 4 * width, depth)), pl.BlockSpec((1, 8, 128), lambda i: (i, 0, 0))],
        out_shape=[
            jax.ShapeDtypeStruct((devices, 4 * width, depth), jnp.bfloat16),
            jax.ShapeDtypeStruct((local_heads, 8, 128), jnp.float32),
        ],
        scratch_shapes=[pltpu.VMEM((capacity, depth), jnp.float32)] * 2,
        name="attend",
    )(sink_logits, recv)
    back = lax.all_to_all(result, "head", split_axis=0, concat_axis=0, tiled=True)
    sink_grad = terms[:, 0, 0]
    groups = lax.axis_size("dp")
    mine = sink_grad
    for shift in range(1, groups):
        sink_grad = sink_grad + lax.ppermute(mine, "dp", [(i, (i + shift) % groups) for i in range(groups)])
    chunk = min(512, rows)
    column = pl.BlockSpec((chunk, 1), lambda i: (i, 0))
    matrix = pl.BlockSpec((chunk, depth), lambda i: (i, 0))
    mixed, dq, dk, dv, gate_sum = pl.pallas_call(
        functools.partial(unpack_kernel, width),
        grid=(rows // chunk,),
        in_specs=[column, column, matrix, whole((devices, 4 * width, depth))],
        out_specs=[matrix] * 4 + [column],
        out_shape=[jax.ShapeDtypeStruct((rows, depth), jnp.bfloat16)] * 4
        + [jax.ShapeDtypeStruct((rows, 1), jnp.float32)],
        name="unpack",
    )(target.reshape(rows, 1), gate_probs.reshape(rows, 1), out_grad.reshape(rows, depth), back)
    gate_sum = gate_sum.reshape(tokens, slots)
    gate_grad = gate_probs * (gate_sum - jnp.sum(gate_probs * gate_sum, axis=-1, keepdims=True))
    shape = query_slots.shape
    return (
        mixed.reshape(shape),
        dq.reshape(shape),
        dk.reshape(shape),
        dv.reshape(shape),
        gate_grad[None],
        sink_grad,
    )


def solution(mesh):
    wide, narrow = P("dp", "head", None, None), P("dp", "head", None)
    return jax.shard_map(
        per_device,
        mesh=mesh,
        in_specs=(narrow, wide, wide, wide, narrow, P("head"), wide),
        out_specs=(wide, wide, wide, wide, narrow, P("head")),
        check_vma=False,
    )
```

```python
import functools
import math

import jax
import jax.numpy as jnp
from jax import lax
from jax.experimental import pallas as pl
from jax.experimental.pallas import tpu as pltpu
from jax.sharding import PartitionSpec as P


SLOT = 32
INFO = 16
MASKED = -1e30


def dot(a, b, dims):
    return lax.dot_general(a, b, (dims, ((), ())), preferred_element_type=jnp.float32)


def position(half):
    index = lax.axis_index("head")
    return index % half, index >= half


def pack_kernel(half, group, first, *refs):
    if first:
        ids_ref, q_ref, k_ref, v_ref, c_ref = refs[:5]
        sends, crosses = refs[5 : 5 + half], refs[5 + half : 5 + 2 * half]
        target_ref, count_ref = refs[-2:]
    else:
        target_ref, count_ref, q_ref, k_ref, v_ref, c_ref = refs[:6]
        sends = refs[6 : 6 + half]
    place, upper = position(half)
    rows = target_ref.shape[1]
    heads = count_ref.shape[0]
    width = group * SLOT
    slots = half * width
    home = 2 * group

    if first:
        before = jnp.where(
            lax.broadcasted_iota(jnp.int32, (128, 128), 0) < lax.broadcasted_iota(jnp.int32, (128, 128), 1), 1.0, 0.0
        ).astype(jnp.bfloat16)
        running = jnp.zeros((heads, 1), jnp.float32)
        for start in range(0, rows, 128):
            ids = ids_ref[:, start : start + 128]
            named = jnp.where(lax.broadcasted_iota(jnp.int32, (heads, 128), 0) == ids, 1.0, 0.0)
            earlier = dot(named.astype(jnp.bfloat16), before, ((1,), (0,))) + running
            slot = jnp.sum(named * earlier, axis=0, keepdims=True).astype(jnp.int32)
            message = (ids // home) ^ place
            late = 1 - (ids % home) // group
            target_ref[:, start : start + 128] = late * slots + message * width + (ids % group) * SLOT + slot
            running = running + jnp.sum(named, axis=1, keepdims=True)
        count_ref[...] = jnp.broadcast_to(running, (heads, 128))

    def picking(chosen):
        row = lax.broadcasted_iota(jnp.int32, (slots, rows), 0) + (1 - chosen) * slots
        return jnp.where(row == target_ref[...], 1.0, 0.0).astype(jnp.bfloat16)

    def counts(chosen):
        line = lax.broadcasted_iota(jnp.int32, (half * INFO, heads), 0)
        wanted = ((line // INFO) ^ place) * home + chosen * group + line % INFO
        wanted = jnp.where(line % INFO < group, wanted, -1)
        take = jnp.where(wanted == lax.broadcasted_iota(jnp.int32, (half * INFO, heads), 1), 1.0, 0.0)
        return dot(take.astype(jnp.bfloat16), count_ref[...].astype(jnp.bfloat16), ((1,), (0,))).astype(jnp.bfloat16)

    def place_pair(pick, left, right, outs, left_part, right_part):
        res = dot(pick, jnp.concatenate([left[...], right[...]], axis=1), ((1,), (0,))).astype(jnp.bfloat16)
        for i, out in enumerate(outs):
            piece = res[i * width : (i + 1) * width]
            out[left_part * width : (left_part + 1) * width] = piece[:, :128]
            out[right_part * width : (right_part + 1) * width] = piece[:, 128:]

    chosen = 1 if first else 0
    pick = picking(chosen)
    place_pair(pick, q_ref, c_ref, sends, 0, 3)
    place_pair(pick, k_ref, v_ref, sends, 1, 2)
    info = counts(chosen)
    for i, out in enumerate(sends):
        out[4 * width :] = info[i * INFO : (i + 1) * INFO]
    if first:

        @pl.when(upper)
        def _():
            for send, cross in zip(sends, crosses):
                cross[:width] = send[:width]
                cross[width : 2 * width] = send[3 * width : 4 * width]

        @pl.when(jnp.logical_not(upper))
        def _():
            place_pair(picking(0), k_ref, v_ref, crosses, 0, 1)

        info = counts(0)
        for i, cross in enumerate(crosses):
            cross[2 * width :] = info[i * INFO : (i + 1) * INFO]


def gather_rows(messages, part, head, width):
    start = pl.multiple_of(part * width + head * SLOT, SLOT)
    return jnp.concatenate([ref[pl.ds(start, SLOT), :] for ref in messages], axis=0)


def put_rows(messages, part, head, width, value):
    start = pl.multiple_of(part * width + head * SLOT, SLOT)
    for i, ref in enumerate(messages):
        ref[pl.ds(start, SLOT), :] = value[i * SLOT : (i + 1) * SLOT].astype(ref.dtype)


def dead_bias(messages, start, head, size):
    pieces = []
    for ref in messages:
        info = ref[start : start + INFO, :].astype(jnp.float32)
        line = lax.broadcasted_iota(jnp.int32, info.shape, 0)
        count = jnp.sum(jnp.where(line == head, info, 0.0), axis=0, keepdims=True)
        slot = lax.broadcasted_iota(jnp.int32, (SLOT, 128), 0).astype(jnp.float32)
        pieces.append(jnp.where(slot < count, 0.0, MASKED))
    bias = jnp.concatenate(pieces, axis=0)
    return jnp.concatenate([bias] * (size // 128), axis=1)


def causal(size, place):
    def order(axis):
        row = lax.broadcasted_iota(jnp.int32, (size, size), axis)
        return ((row // SLOT) ^ place) * SLOT + row % SLOT

    return order(0) <= order(1)


def column_sum(parts):
    return sum(jnp.sum(part, axis=0, keepdims=True) for part in parts)


def statistics(query, cot, keys, sink):
    scale = 1.0 / math.sqrt(query.shape[-1])
    scores = [mask(scale * dot(key, query, ((1,), (1,)))) for key, _, mask in keys]
    top = functools.reduce(jnp.maximum, [jnp.max(score, axis=0, keepdims=True) for score in scores])
    sink_part = None
    if sink is not None:
        top = jnp.maximum(top, sink)
        sink_part = jnp.exp(sink - top)
    powers = [jnp.exp(score - top) for score in scores]
    run = column_sum(powers)
    if sink is not None:
        run = run + sink_part
    inv = 1.0 / run
    dprobs = [dot(value, cot, ((1,), (1,))) for _, value, _ in keys]
    delta = inv * column_sum([power * dprob for power, dprob in zip(powers, dprobs)])
    return powers, dprobs, top + jnp.log(run), inv, delta, sink_part


def attend(query, cot, keys, sink, other=None):
    scale = 1.0 / math.sqrt(query.shape[-1])
    powers, dprobs, lse, inv, delta, sink_part = statistics(query, cot, keys, sink)
    if other is not None:
        other_lse, other_delta = other
        top = jnp.maximum(lse, other_lse)
        mine, theirs = jnp.exp(lse - top), jnp.exp(other_lse - top)
        share = 1.0 / (mine + theirs)
        delta = (mine * delta + theirs * other_delta) * share
        inv = inv * (mine * share)
    head_out = query_grad = 0.0
    grads = []
    for power, dprob, (key, value, _) in zip(powers, dprobs, keys):
        prob = power * inv
        weights = prob.astype(jnp.bfloat16)
        dscore = (prob * (dprob - delta)).astype(jnp.bfloat16)
        head_out = head_out + dot(value, weights, ((0,), (0,)))
        query_grad = query_grad + dot(key, dscore, ((0,), (0,)))
        grads.append((scale * dot(dscore, query, ((1,), (0,))), dot(weights, cot, ((1,), (0,)))))
    term = 0.0 if sink_part is None else -jnp.sum(sink_part * inv * delta, axis=1, keepdims=True)
    return head_out.T, (scale * query_grad).T, grads, term


def own_keys(messages, head, width, size, mask):
    bias = dead_bias(messages, 4 * width, head, size)
    key, value = (gather_rows(messages, part, head, width) for part in (1, 2))
    if mask is None:
        return key, value, lambda score: score + bias
    return key, value, lambda score: jnp.where(mask, score + bias, MASKED)


def split_kernel(half, group, sink_ref, *refs):
    owns, crosses, stat_ref = refs[:half], refs[half : 2 * half], refs[2 * half]
    place, upper = position(half)
    head = pl.program_id(0)
    width, size = group * SLOT, half * SLOT

    def write(query, cot, mask, sink):
        _, _, lse, _, delta, _ = statistics(query, cot, [own_keys(owns, head, width, size, mask)], sink)
        stat_ref[0] = jnp.concatenate([lse, delta, jnp.zeros((6, size), jnp.float32)], axis=0)

    @pl.when(upper)
    def _():
        write(
            gather_rows(owns, 0, head, width), gather_rows(owns, 3, head, width), causal(size, place), sink_ref[head]
        )

    @pl.when(jnp.logical_not(upper))
    def _():
        write(gather_rows(crosses, 0, head, width), gather_rows(crosses, 1, head, width), None, None)


def late_kernel(half, group, sink_ref, *refs):
    stat_ref, owns, crosses = refs[0], refs[1 : 1 + half], refs[1 + half : 1 + 2 * half]
    outs, cross_outs, term_ref = refs[1 + 2 * half : 1 + 3 * half], refs[1 + 3 * half : 1 + 4 * half], refs[1 + 4 * half]
    place, upper = position(half)
    head = pl.program_id(0)
    width, size = group * SLOT, half * SLOT
    sink = sink_ref[head]
    mask = causal(size, place)
    query, cot = gather_rows(owns, 0, head, width), gather_rows(owns, 3, head, width)
    keys = own_keys(owns, head, width, size, mask)
    other = (stat_ref[0, 0:1, :], stat_ref[0, 1:2, :])

    def finish(head_out, query_grad, key_grad, value_grad, term):
        for part, value in enumerate((head_out, query_grad, key_grad, value_grad)):
            put_rows(outs, part, head, width, value)
        term_ref[0] = jnp.broadcast_to(term, (8, 128))

    @pl.when(upper)
    def _():
        head_out, query_grad, grads, term = attend(query, cot, [keys], sink, other)
        finish(head_out, query_grad, grads[0][0], grads[0][1], term)

    @pl.when(jnp.logical_not(upper))
    def _():
        head_out, query_grad, grads, term = attend(query, cot, [keys], sink)
        far_query, far_cot = gather_rows(crosses, 0, head, width), gather_rows(crosses, 1, head, width)
        far_keys = own_keys(owns, head, width, size, None)
        far_out, far_grad, more, _ = attend(far_query, far_cot, [far_keys], None, other)
        finish(head_out, query_grad, grads[0][0] + more[0][0], grads[0][1] + more[0][1], term)
        put_rows(cross_outs, 0, head, width, far_out)
        put_rows(cross_outs, 1, head, width, far_grad)


def early_kernel(half, group, sink_ref, *refs):
    owns, crosses, passed = refs[:half], refs[half : 2 * half], refs[2 * half : 3 * half]
    outs, cross_outs, term_ref = refs[3 * half : 4 * half], refs[4 * half : 5 * half], refs[5 * half]
    place, upper = position(half)
    head = pl.program_id(0)
    width, size = group * SLOT, half * SLOT
    sink = sink_ref[head]
    query, cot = gather_rows(owns, 0, head, width), gather_rows(owns, 3, head, width)
    keys = own_keys(owns, head, width, size, causal(size, place))

    def finish(head_out, query_grad, grads, term):
        for part, value in enumerate((head_out, query_grad) + grads[0]):
            put_rows(outs, part, head, width, value)
        term_ref[0] = jnp.broadcast_to(term, (8, 128))

    @pl.when(upper)
    def _():
        bias = dead_bias(crosses, 2 * width, head, size)
        far = (
            gather_rows(crosses, 0, head, width),
            gather_rows(crosses, 1, head, width),
            lambda score: score + bias,
        )
        head_out, query_grad, grads, term = attend(query, cot, [keys, far], sink)
        finish(head_out, query_grad, grads, term)
        put_rows(cross_outs, 0, head, width, grads[1][0])
        put_rows(cross_outs, 1, head, width, grads[1][1])

    @pl.when(jnp.logical_not(upper))
    def _():
        finish(*attend(query, cot, [keys], sink))
        for old, new in zip(passed, cross_outs):
            for part in range(2):
                start = pl.multiple_of(part * width + head * SLOT, SLOT)
                new[pl.ds(start, SLOT), :] = old[pl.ds(start, SLOT), :]


def unpack_kernel(half, group, target_ref, gate_ref, grad_ref, *refs):
    lates, earlies, crosses = refs[:half], refs[half : 2 * half], refs[2 * half : 3 * half]
    mixed_ref, dq_ref, dk_ref, dv_ref, sum_ref = refs[3 * half :]
    _, upper = position(half)
    chunk = target_ref.shape[0]
    width = group * SLOT
    slots = half * width
    target = target_ref[...]

    def picking(size, start):
        return jnp.where(lax.broadcasted_iota(jnp.int32, (chunk, size), 1) + start == target, 1.0, 0.0).astype(
            jnp.bfloat16
        )

    def table(messages, part):
        return jnp.concatenate([ref[part * width : (part + 1) * width] for ref in messages], axis=0)

    pick = picking(2 * slots, 0)

    def both(first):
        parts = [
            jnp.concatenate([table(lates, part), table(earlies, part)], axis=0) for part in (first, first + 1)
        ]
        return dot(pick, jnp.concatenate(parts, axis=1), ((1,), (0,)))

    far = dot(
        picking(slots, jnp.where(upper, 0, slots)),
        jnp.concatenate([table(crosses, 0), table(crosses, 1)], axis=1),
        ((1,), (0,)),
    )
    forward = both(0) + jnp.where(upper, far, 0.0)
    token_out = forward[:, :128]
    mixed_ref[...] = (gate_ref[...] * token_out).astype(jnp.bfloat16)
    sum_ref[...] = jnp.sum(grad_ref[...].astype(jnp.float32) * token_out, axis=1, keepdims=True)
    dq_ref[...] = forward[:, 128:].astype(jnp.bfloat16)
    backward = both(2) + jnp.where(upper, 0.0, far)
    dk_ref[...] = backward[:, :128].astype(jnp.bfloat16)
    dv_ref[...] = backward[:, 128:].astype(jnp.bfloat16)


def whole(shape):
    return pl.BlockSpec(shape, lambda *_: (0,) * len(shape))


def per_device(head_ids, query_slots, key_slots, value_slots, gate_logits, sink_logits, out_grad):
    devices = lax.axis_size("head")
    half = devices // 2
    group = sink_logits.shape[0]
    heads = group * devices
    tokens, slots = head_ids.shape[1:]
    depth = query_slots.shape[-1]
    rows = tokens * slots
    width, size = group * SLOT, half * SLOT
    upper = lax.axis_index("head") >= half
    bf16 = jnp.bfloat16
    smem = pl.BlockSpec(memory_space=pltpu.SMEM)

    def exchange(message, i, cross):
        return lax.ppermute(
            message, "head", [(d, (d ^ i) if not cross else (d ^ i ^ half)) for d in range(devices)]
        )

    def exchange_all(messages):
        return [messages[0]] + [exchange(messages[i], i, False) for i in range(1, half)]

    def cross_all(messages):
        return [exchange(messages[i], i, True) for i in range(half)]

    to_home = [[(d, d // 2 + half * ((d + turn) % 2)) for d in range(devices)] for turn in range(2)]
    near, far = (lax.ppermute(sink_logits, "head", pairs) for pairs in to_home)
    sink_early, sink_late = jnp.where(upper, far, near), jnp.where(upper, near, far)

    ids = head_ids.reshape(1, rows)
    gate_probs = jax.nn.softmax(gate_logits[0], axis=-1)
    cotangent = (gate_probs[:, :, None] * out_grad[0].astype(jnp.float32)).astype(bf16)
    flat = [item.reshape(rows, depth) for item in (query_slots, key_slots, value_slots, cotangent)]
    message = jax.ShapeDtypeStruct((4 * width + INFO, depth), bf16)
    crossing = jax.ShapeDtypeStruct((2 * width + INFO, depth), bf16)
    result = jax.ShapeDtypeStruct((4 * width, depth), bf16)
    cross_result = jax.ShapeDtypeStruct((2 * width, depth), bf16)
    *packed, target, count = pl.pallas_call(
        functools.partial(pack_kernel, half, group, True),
        out_shape=[message] * half
        + [crossing] * half
        + [jax.ShapeDtypeStruct((1, rows), jnp.int32), jax.ShapeDtypeStruct((heads, 128), jnp.float32)],
        name="pack_late",
    )(ids, *flat)
    crosses = cross_all(packed[half:])
    lates = exchange_all(packed[:half])
    packed = pl.pallas_call(
        functools.partial(pack_kernel, half, group, False), out_shape=[message] * half, name="pack_early"
    )(target, count, *flat)
    earlies = exchange_all(packed)

    stats = pl.pallas_call(
        functools.partial(split_kernel, half, group),
        grid=(group,),
        in_specs=[smem] + [whole(message.shape)] * half + [whole(crossing.shape)] * half,
        out_specs=pl.BlockSpec((1, 8, size), lambda h: (h, 0, 0)),
        out_shape=jax.ShapeDtypeStruct((group, 8, size), jnp.float32),
        name="split",
    )(sink_late, *lates, *crosses)
    stats = exchange(stats, 0, True)
    term_spec = pl.BlockSpec((1, 8, 128), lambda h: (h, 0, 0))
    term_shape = jax.ShapeDtypeStruct((group, 8, 128), jnp.float32)
    *results, late_terms = pl.pallas_call(
        functools.partial(late_kernel, half, group),
        grid=(group,),
        in_specs=[smem, pl.BlockSpec((1, 8, size), lambda h: (h, 0, 0))]
        + [whole(message.shape)] * half
        + [whole(crossing.shape)] * half,
        out_specs=[whole(result.shape)] * half + [whole(cross_result.shape)] * half + [term_spec],
        out_shape=[result] * half + [cross_result] * half + [term_shape],
        name="late",
    )(sink_late, stats, *lates, *crosses)
    late_back = exchange_all(results[:half])
    *results, early_terms = pl.pallas_call(
        functools.partial(early_kernel, half, group),
        grid=(group,),
        in_specs=[smem]
        + [whole(message.shape)] * half
        + [whole(crossing.shape)] * half
        + [whole(cross_result.shape)] * half,
        out_specs=[whole(result.shape)] * half + [whole(cross_result.shape)] * half + [term_spec],
        out_shape=[result] * half + [cross_result] * half + [term_shape],
        name="early",
    )(sink_early, *earlies, *crosses, *results[half:])
    cross_back = cross_all(results[half:])
    early_back = exchange_all(results[:half])

    late_terms, early_terms = late_terms[:, 0, 0], early_terms[:, 0, 0]
    near, far = jnp.where(upper, late_terms, early_terms), jnp.where(upper, early_terms, late_terms)
    sink_grad = sum(
        lax.ppermute(item, "head", [(to, d) for d, to in pairs]) for item, pairs in zip((near, far), to_home)
    )
    groups = lax.axis_size("dp")
    mine = sink_grad
    for shift in range(1, groups):
        sink_grad = sink_grad + lax.ppermute(mine, "dp", [(i, (i + shift) % groups) for i in range(groups)])

    chunk = min(512, rows)
    column = pl.BlockSpec((chunk, 1), lambda i: (i, 0))
    matrix = pl.BlockSpec((chunk, depth), lambda i: (i, 0))
    mixed, dq, dk, dv, gate_sum = pl.pallas_call(
        functools.partial(unpack_kernel, half, group),
        grid=(rows // chunk,),
        in_specs=[column, column, matrix] + [whole(result.shape)] * (2 * half) + [whole(cross_result.shape)] * half,
        out_specs=[matrix] * 4 + [column],
        out_shape=[jax.ShapeDtypeStruct((rows, depth), bf16)] * 4 + [jax.ShapeDtypeStruct((rows, 1), jnp.float32)],
        name="unpack",
    )(
        target.reshape(rows, 1),
        gate_probs.reshape(rows, 1),
        out_grad.reshape(rows, depth),
        *late_back,
        *early_back,
        *cross_back,
    )
    gate_sum = gate_sum.reshape(tokens, slots)
    gate_grad = gate_probs * (gate_sum - jnp.sum(gate_probs * gate_sum, axis=-1, keepdims=True))
    shape = query_slots.shape
    return (
        mixed.reshape(shape),
        dq.reshape(shape),
        dk.reshape(shape),
        dv.reshape(shape),
        gate_grad[None],
        sink_grad,
    )


def solution(mesh):
    wide, narrow = P("dp", "head", None, None), P("dp", "head", None)
    return jax.shard_map(
        per_device,
        mesh=mesh,
        in_specs=(narrow, wide, wide, wide, narrow, P("head"), wide),
        out_specs=(wide, wide, wide, wide, narrow, P("head")),
        check_vma=False,
    )
```

```python
import functools
import math

import jax
import jax.numpy as jnp
from jax import lax
from jax.experimental import pallas as pl
from jax.experimental.pallas import tpu as pltpu
from jax.sharding import PartitionSpec as P


SLOT = 32
INFO = 16
MASKED = -1e30


def dot(a, b, dims):
    return lax.dot_general(a, b, (dims, ((), ())), preferred_element_type=jnp.float32)


def position(half):
    index = lax.axis_index("head")
    return index % half, index >= half


def pack_kernel(half, group, first, *refs):
    chips = half // 2
    if first:
        ids_refs, own, mate = refs[:2], refs[2:6], refs[6:10]
        sends, crosses = refs[10 : 10 + chips], refs[10 + chips : 10 + 2 * chips]
        pack_ref, unpack_ref, count_ref = refs[-3:]
    else:
        pack_ref, count_ref, own, mate = refs[0], refs[1], refs[2:6], refs[6:10]
        sends = refs[10 : 10 + chips]
    place, upper = position(half)
    chip, core = place // 2, place % 2
    rows = pack_ref.shape[1]
    heads = count_ref.shape[0] // 2
    width = group * SLOT
    slots = chips * width
    home_heads = 2 * group

    if first:
        before = jnp.where(
            lax.broadcasted_iota(jnp.int32, (128, 128), 0) < lax.broadcasted_iota(jnp.int32, (128, 128), 1), 1.0, 0.0
        ).astype(jnp.bfloat16)
        for source, ids_ref in enumerate(ids_refs):
            running = jnp.zeros((heads, 1), jnp.float32)
            for start in range(0, rows, 128):
                ids = ids_ref[:, start : start + 128]
                named = jnp.where(lax.broadcasted_iota(jnp.int32, (heads, 128), 0) == ids, 1.0, 0.0)
                earlier = dot(named.astype(jnp.bfloat16), before, ((1,), (0,))) + running
                slot = jnp.sum(named * earlier, axis=0, keepdims=True).astype(jnp.int32)
                home = ids // home_heads
                late = 1 - (ids % home_heads) // group
                slot = slot + (ids % group) * SLOT
                pack_ref[source : source + 1, start : start + 128] = jnp.where(
                    home % 2 == core, late * slots + ((home // 2) ^ chip) * width + slot, -1
                )
                if source == 0:
                    unpack_ref[:, start : start + 128] = late * (2 * slots) + (home ^ place) * width + slot
                running = running + jnp.sum(named, axis=1, keepdims=True)
            from_core = core if source == 0 else 1 - core
            count_ref[pl.ds(pl.multiple_of(from_core * heads, heads), heads), :] = jnp.broadcast_to(
                running, (heads, 128)
            )

    def counts(chosen):
        line = lax.broadcasted_iota(jnp.int32, (chips * INFO, 2 * heads), 0)
        inner = line % INFO
        wanted = (2 * ((line // INFO) ^ chip) + core) * home_heads + chosen * group + inner % group
        wanted = jnp.where(inner < 2 * group, wanted + (inner // group) * heads, -1)
        take = jnp.where(wanted == lax.broadcasted_iota(jnp.int32, (chips * INFO, 2 * heads), 1), 1.0, 0.0)
        return dot(take.astype(jnp.bfloat16), count_ref[...].astype(jnp.bfloat16), ((1,), (0,))).astype(jnp.bfloat16)

    def place_pairs(chosen, pairs, outs):
        for source, refs in enumerate((own, mate)):
            row = lax.broadcasted_iota(jnp.int32, (slots, rows), 0) + (1 - chosen) * slots
            pick = jnp.where(row == pack_ref[source : source + 1, :], 1.0, 0.0).astype(jnp.bfloat16)
            from_core = core if source == 0 else 1 - core
            for left, right, left_part, right_part in pairs:
                both = jnp.concatenate([refs[left][...], refs[right][...]], axis=1)
                res = dot(pick, both, ((1,), (0,))).astype(jnp.bfloat16)
                for i, out in enumerate(outs):
                    for head in range(group):
                        piece = res[i * width + head * SLOT : i * width + (head + 1) * SLOT]
                        for part, value in ((left_part, piece[:, :128]), (right_part, piece[:, 128:])):
                            start = pl.multiple_of(2 * (part * width + head * SLOT) + from_core * SLOT, SLOT)
                            out[pl.ds(start, SLOT), :] = value

    chosen = 1 if first else 0
    place_pairs(chosen, ((0, 3, 0, 3), (1, 2, 1, 2)), sends)
    info = counts(chosen)
    for i, out in enumerate(sends):
        out[8 * width :] = info[i * INFO : (i + 1) * INFO]
    if first:

        @pl.when(upper)
        def _():
            for send, cross in zip(sends, crosses):
                cross[: 2 * width] = send[: 2 * width]
                cross[2 * width : 4 * width] = send[6 * width : 8 * width]

        @pl.when(jnp.logical_not(upper))
        def _():
            place_pairs(0, ((1, 2, 0, 1),), crosses)

        info = counts(0)
        for i, cross in enumerate(crosses):
            cross[4 * width :] = info[i * INFO : (i + 1) * INFO]


def gather_rows(messages, part, head, width):
    start = 2 * (part * width + head * SLOT)
    return jnp.concatenate([ref[start : start + 2 * SLOT] for ref in messages], axis=0)


def put_rows(messages, part, head, width, core, value):
    start = part * width + head * SLOT
    value = value.astype(messages[0].dtype)
    for chip in range(len(messages) // 2):
        pieces = [value[(2 * chip + side) * SLOT : (2 * chip + side + 1) * SLOT] for side in range(2)]
        for side in range(2):
            messages[2 * chip + side][start : start + SLOT] = jnp.where(core == 0, pieces[side], pieces[1 - side])


def dead_bias(messages, start, head, group, size):
    pieces = []
    slot = lax.broadcasted_iota(jnp.int32, (SLOT, 128), 0).astype(jnp.float32)
    for ref in messages:
        info = ref[start : start + INFO, :].astype(jnp.float32)
        for core in range(2):
            line = core * group + head
            pieces.append(jnp.where(slot < info[line : line + 1], 0.0, MASKED))
    bias = jnp.concatenate(pieces, axis=0)
    return jnp.concatenate([bias] * (size // 128), axis=1)


def causal(size, place):
    def order(axis):
        row = lax.broadcasted_iota(jnp.int32, (size, size), axis)
        return ((row // (2 * SLOT)) ^ (place // 2)) * (2 * SLOT) + row % (2 * SLOT)

    return order(0) <= order(1)


def column_sum(parts):
    return sum(jnp.sum(part, axis=0, keepdims=True) for part in parts)


def statistics(query, cot, keys, sink):
    scale = 1.0 / math.sqrt(query.shape[-1])
    scores = [mask(scale * dot(key, query, ((1,), (1,)))) for key, _, mask in keys]
    top = functools.reduce(jnp.maximum, [jnp.max(score, axis=0, keepdims=True) for score in scores])
    sink_part = None
    if sink is not None:
        top = jnp.maximum(top, sink)
        sink_part = jnp.exp(sink - top)
    powers = [jnp.exp(score - top) for score in scores]
    run = column_sum(powers)
    if sink is not None:
        run = run + sink_part
    inv = 1.0 / run
    dprobs = [dot(value, cot, ((1,), (1,))) for _, value, _ in keys]
    delta = inv * column_sum([power * dprob for power, dprob in zip(powers, dprobs)])
    return powers, dprobs, top + jnp.log(run), inv, delta, sink_part


def attend(query, cot, keys, sink, other=None):
    scale = 1.0 / math.sqrt(query.shape[-1])
    powers, dprobs, lse, inv, delta, sink_part = statistics(query, cot, keys, sink)
    if other is not None:
        other_lse, other_delta = other
        top = jnp.maximum(lse, other_lse)
        mine, theirs = jnp.exp(lse - top), jnp.exp(other_lse - top)
        share = 1.0 / (mine + theirs)
        delta = (mine * delta + theirs * other_delta) * share
        inv = inv * (mine * share)
    head_out = query_grad = 0.0
    grads = []
    for power, dprob, (key, value, _) in zip(powers, dprobs, keys):
        prob = power * inv
        weights = prob.astype(jnp.bfloat16)
        dscore = (prob * (dprob - delta)).astype(jnp.bfloat16)
        head_out = head_out + dot(value, weights, ((0,), (0,)))
        query_grad = query_grad + dot(key, dscore, ((0,), (0,)))
        grads.append((scale * dot(dscore, query, ((1,), (0,))), dot(weights, cot, ((1,), (0,)))))
    term = 0.0 if sink_part is None else -jnp.sum(sink_part * inv * delta, axis=1, keepdims=True)
    return head_out.T, (scale * query_grad).T, grads, term


def own_keys(messages, head, group, size, mask):
    width = group * SLOT
    bias = dead_bias(messages, 8 * width, head, group, size)
    key, value = (gather_rows(messages, part, head, width) for part in (1, 2))
    if mask is None:
        return key, value, lambda score: score + bias
    return key, value, lambda score: jnp.where(mask, score + bias, MASKED)


def split_kernel(half, group, sink_ref, *refs):
    chips = half // 2
    owns, crosses, stat_ref = refs[:chips], refs[chips : 2 * chips], refs[2 * chips]
    place, upper = position(half)
    width, size = group * SLOT, half * SLOT

    def write(head, query, cot, mask, sink):
        _, _, lse, _, delta, _ = statistics(query, cot, [own_keys(owns, head, group, size, mask)], sink)
        stat_ref[head] = jnp.concatenate([lse, delta, jnp.zeros((6, size), jnp.float32)], axis=0)

    @pl.when(upper)
    def _():
        mask = causal(size, place)
        for head in range(group):
            query, cot = gather_rows(owns, 0, head, width), gather_rows(owns, 3, head, width)
            write(head, query, cot, mask, sink_ref[head])

    @pl.when(jnp.logical_not(upper))
    def _():
        for head in range(group):
            query, cot = gather_rows(crosses, 0, head, width), gather_rows(crosses, 1, head, width)
            write(head, query, cot, None, None)


def late_kernel(half, group, sink_ref, *refs):
    chips = half // 2
    stat_ref, owns, crosses, refs = refs[0], refs[1 : 1 + chips], refs[1 + chips : 1 + half], refs[1 + half :]
    outs, cross_outs, term_ref = refs[:half], refs[half : 2 * half], refs[2 * half]
    place, upper = position(half)
    core = place % 2
    width, size = group * SLOT, half * SLOT
    mask = causal(size, place)

    def finish(head, head_out, query_grad, key_grad, value_grad, term):
        for part, value in enumerate((head_out, query_grad, key_grad, value_grad)):
            put_rows(outs, part, head, width, core, value)
        term_ref[head] = jnp.broadcast_to(term, (8, 128))

    @pl.when(upper)
    def _():
        for head in range(group):
            query, cot = gather_rows(owns, 0, head, width), gather_rows(owns, 3, head, width)
            keys = own_keys(owns, head, group, size, mask)
            other = (stat_ref[head, 0:1, :], stat_ref[head, 1:2, :])
            head_out, query_grad, grads, term = attend(query, cot, [keys], sink_ref[head], other)
            finish(head, head_out, query_grad, grads[0][0], grads[0][1], term)

    @pl.when(jnp.logical_not(upper))
    def _():
        for head in range(group):
            query, cot = gather_rows(owns, 0, head, width), gather_rows(owns, 3, head, width)
            other = (stat_ref[head, 0:1, :], stat_ref[head, 1:2, :])
            keys = own_keys(owns, head, group, size, mask)
            head_out, query_grad, grads, term = attend(query, cot, [keys], sink_ref[head])
            far_query, far_cot = gather_rows(crosses, 0, head, width), gather_rows(crosses, 1, head, width)
            far_keys = own_keys(owns, head, group, size, None)
            far_out, far_grad, more, _ = attend(far_query, far_cot, [far_keys], None, other)
            finish(head, head_out, query_grad, grads[0][0] + more[0][0], grads[0][1] + more[0][1], term)
            put_rows(cross_outs, 0, head, width, core, far_out)
            put_rows(cross_outs, 1, head, width, core, far_grad)


def early_kernel(half, group, sink_ref, *refs):
    chips = half // 2
    owns, crosses, passed, refs = refs[:chips], refs[chips:half], refs[half : 2 * half], refs[2 * half :]
    outs, cross_outs, term_ref = refs[:half], refs[half : 2 * half], refs[2 * half]
    place, upper = position(half)
    core = place % 2
    width, size = group * SLOT, half * SLOT
    mask = causal(size, place)

    def finish(head, head_out, query_grad, grads, term):
        for part, value in enumerate((head_out, query_grad) + grads[0]):
            put_rows(outs, part, head, width, core, value)
        term_ref[head] = jnp.broadcast_to(term, (8, 128))

    def own(head):
        query, cot = gather_rows(owns, 0, head, width), gather_rows(owns, 3, head, width)
        return query, cot, own_keys(owns, head, group, size, mask)

    @pl.when(upper)
    def _():
        for head in range(group):
            query, cot, keys = own(head)
            far_bias = dead_bias(crosses, 4 * width, head, group, size)
            far = (
                gather_rows(crosses, 0, head, width),
                gather_rows(crosses, 1, head, width),
                functools.partial(jnp.add, far_bias),
            )
            head_out, query_grad, grads, term = attend(query, cot, [keys, far], sink_ref[head])
            finish(head, head_out, query_grad, grads, term)
            put_rows(cross_outs, 0, head, width, core, grads[1][0])
            put_rows(cross_outs, 1, head, width, core, grads[1][1])

    @pl.when(jnp.logical_not(upper))
    def _():
        for head in range(group):
            query, cot, keys = own(head)
            finish(head, *attend(query, cot, [keys], sink_ref[head]))
        for old, new in zip(passed, cross_outs):
            new[...] = old[...]


def unpack_kernel(half, group, target_ref, gate_ref, grad_ref, *refs):
    lates, earlies, crosses = refs[:half], refs[half : 2 * half], refs[2 * half : 3 * half]
    mixed_ref, dq_ref, dk_ref, dv_ref, sum_ref = refs[3 * half :]
    _, upper = position(half)
    chunk = target_ref.shape[0]
    width = group * SLOT
    slots = half * width
    target = target_ref[...]

    def picking(size, start):
        return jnp.where(lax.broadcasted_iota(jnp.int32, (chunk, size), 1) + start == target, 1.0, 0.0).astype(
            jnp.bfloat16
        )

    def table(messages, part):
        return jnp.concatenate([ref[part * width : (part + 1) * width] for ref in messages], axis=0)

    pick = picking(2 * slots, 0)

    def both(first):
        parts = [
            jnp.concatenate([table(lates, part), table(earlies, part)], axis=0) for part in (first, first + 1)
        ]
        return dot(pick, jnp.concatenate(parts, axis=1), ((1,), (0,)))

    far = dot(
        picking(slots, jnp.where(upper, 0, slots)),
        jnp.concatenate([table(crosses, 0), table(crosses, 1)], axis=1),
        ((1,), (0,)),
    )
    forward = both(0) + jnp.where(upper, far, 0.0)
    token_out = forward[:, :128]
    mixed_ref[...] = (gate_ref[...] * token_out).astype(jnp.bfloat16)
    sum_ref[...] = jnp.sum(grad_ref[...].astype(jnp.float32) * token_out, axis=1, keepdims=True)
    dq_ref[...] = forward[:, 128:].astype(jnp.bfloat16)
    backward = both(2) + jnp.where(upper, 0.0, far)
    dk_ref[...] = backward[:, :128].astype(jnp.bfloat16)
    dv_ref[...] = backward[:, 128:].astype(jnp.bfloat16)


def whole(shape):
    return pl.BlockSpec(shape, lambda *_: (0,) * len(shape))


def per_device(head_ids, query_slots, key_slots, value_slots, gate_logits, sink_logits, out_grad):
    devices = lax.axis_size("head")
    half = devices // 2
    group = sink_logits.shape[0]
    heads = group * devices
    tokens, slots = head_ids.shape[1:]
    depth = query_slots.shape[-1]
    rows = tokens * slots
    width, size = group * SLOT, half * SLOT
    upper = lax.axis_index("head") >= half
    bf16 = jnp.bfloat16
    smem = pl.BlockSpec(memory_space=pltpu.SMEM)

    def exchange(message, i, cross):
        return lax.ppermute(
            message, "head", [(d, (d ^ i) if not cross else (d ^ i ^ half)) for d in range(devices)]
        )

    def exchange_all(messages):
        return [messages[0]] + [exchange(messages[i], i, False) for i in range(1, half)]

    def cross_all(messages):
        return [exchange(messages[i], i, True) for i in range(half)]

    to_home = [[(d, d // 2 + half * ((d + turn) % 2)) for d in range(devices)] for turn in range(2)]
    near, far = (lax.ppermute(sink_logits, "head", pairs) for pairs in to_home)
    sink_early, sink_late = jnp.where(upper, far, near), jnp.where(upper, near, far)

    def mate(value):
        return lax.ppermute(value, "head", [(d, d ^ 1) for d in range(devices)])

    flat = [item.reshape(rows, depth) for item in (query_slots, key_slots, value_slots)]
    ids = head_ids.reshape(1, rows)
    mate_ids = mate(ids)
    mate_flat = [mate(item) for item in flat]
    gate_probs = jax.nn.softmax(gate_logits[0], axis=-1)
    cotangent = (gate_probs[:, :, None] * out_grad[0].astype(jnp.float32)).astype(bf16).reshape(rows, depth)
    flat.append(cotangent)
    mate_flat.append(mate(cotangent))
    chips = half // 2
    message = jax.ShapeDtypeStruct((8 * width + INFO, depth), bf16)
    crossing = jax.ShapeDtypeStruct((4 * width + INFO, depth), bf16)
    result = jax.ShapeDtypeStruct((4 * width, depth), bf16)
    cross_result = jax.ShapeDtypeStruct((2 * width, depth), bf16)
    *packed, pack_target, target, count = pl.pallas_call(
        functools.partial(pack_kernel, half, group, True),
        out_shape=[message] * chips
        + [crossing] * chips
        + [
            jax.ShapeDtypeStruct((2, rows), jnp.int32),
            jax.ShapeDtypeStruct((1, rows), jnp.int32),
            jax.ShapeDtypeStruct((2 * heads, 128), jnp.float32),
        ],
        name="pack_late",
    )(ids, mate_ids, *flat, *mate_flat)
    crosses = [exchange(packed[chips + i], 2 * i, True) for i in range(chips)]
    lates = [packed[0]] + [exchange(packed[i], 2 * i, False) for i in range(1, chips)]
    packed = pl.pallas_call(
        functools.partial(pack_kernel, half, group, False), out_shape=[message] * chips, name="pack_early"
    )(pack_target, count, *flat, *mate_flat)
    earlies = [packed[0]] + [exchange(packed[i], 2 * i, False) for i in range(1, chips)]

    vmem = pl.BlockSpec(memory_space=pltpu.VMEM)
    stats = pl.pallas_call(
        functools.partial(split_kernel, half, group),
        in_specs=[smem] + [vmem] * half,
        out_shape=jax.ShapeDtypeStruct((group, 8, size), jnp.float32),
        name="split",
    )(sink_late, *lates, *crosses)
    stats = exchange(stats, 0, True)
    answer = [result] * half + [cross_result] * half + [jax.ShapeDtypeStruct((group, 8, 128), jnp.float32)]
    *results, late_terms = pl.pallas_call(
        functools.partial(late_kernel, half, group),
        in_specs=[smem] + [vmem] * (1 + half),
        out_shape=answer,
        name="late",
    )(sink_late, stats, *lates, *crosses)
    late_back = exchange_all(results[:half])
    *results, early_terms = pl.pallas_call(
        functools.partial(early_kernel, half, group),
        in_specs=[smem] + [vmem] * (2 * half),
        out_shape=answer,
        name="early",
    )(sink_early, *earlies, *crosses, *results[half:])
    cross_back = cross_all(results[half:])
    early_back = exchange_all(results[:half])

    late_terms, early_terms = late_terms[:, 0, 0], early_terms[:, 0, 0]
    near, far = jnp.where(upper, late_terms, early_terms), jnp.where(upper, early_terms, late_terms)
    sink_grad = sum(
        lax.ppermute(item, "head", [(to, d) for d, to in pairs]) for item, pairs in zip((near, far), to_home)
    )
    groups = lax.axis_size("dp")
    mine = sink_grad
    for shift in range(1, groups):
        sink_grad = sink_grad + lax.ppermute(mine, "dp", [(i, (i + shift) % groups) for i in range(groups)])

    chunk = min(512, rows)
    column = pl.BlockSpec((chunk, 1), lambda i: (i, 0))
    matrix = pl.BlockSpec((chunk, depth), lambda i: (i, 0))
    mixed, dq, dk, dv, gate_sum = pl.pallas_call(
        functools.partial(unpack_kernel, half, group),
        grid=(rows // chunk,),
        in_specs=[column, column, matrix] + [whole(result.shape)] * (2 * half) + [whole(cross_result.shape)] * half,
        out_specs=[matrix] * 4 + [column],
        out_shape=[jax.ShapeDtypeStruct((rows, depth), bf16)] * 4 + [jax.ShapeDtypeStruct((rows, 1), jnp.float32)],
        name="unpack",
    )(
        target.reshape(rows, 1),
        gate_probs.reshape(rows, 1),
        out_grad.reshape(rows, depth),
        *late_back,
        *early_back,
        *cross_back,
    )
    gate_sum = gate_sum.reshape(tokens, slots)
    gate_grad = gate_probs * (gate_sum - jnp.sum(gate_probs * gate_sum, axis=-1, keepdims=True))
    shape = query_slots.shape
    return (
        mixed.reshape(shape),
        dq.reshape(shape),
        dk.reshape(shape),
        dv.reshape(shape),
        gate_grad[None],
        sink_grad,
    )


def solution(mesh):
    wide, narrow = P("dp", "head", None, None), P("dp", "head", None)
    return jax.shard_map(
        per_device,
        mesh=mesh,
        in_specs=(narrow, wide, wide, wide, narrow, P("head"), wide),
        out_specs=(wide, wide, wide, wide, narrow, P("head")),
        check_vma=False,
    )
```
